32 devices in a mesh: section: 2 (over core), fsdp: 16 (over z, y, x).
Axes of the slice: x: 2, y: 2, z: 4, core: 2. Of those that a mesh axis runs over, the one named last changes fastest.
Arguments:
- block_input: bfloat16 [4, 16, 7, 14, 512], P(None, 'fsdp'), may hold values from -6 to 6
- cotangent: bfloat16 [4, 16, 7, 14, 512], P(None, 'fsdp'), may hold values from -6 to 6
- qkv_weight: bfloat16 [2, 512, 1536], P('section', 'fsdp'), may hold values from -0.25 to 0.25
- proj_weight: bfloat16 [2, 512, 512], P('section', 'fsdp'), may hold values from -2 to 2
- fc1_weight: bfloat16 [2, 512, 2048], P('section', 'fsdp'), may hold values from -0.25 to 0.25
- fc2_weight: bfloat16 [2, 2048, 512], P('section', 'fsdp'), may hold values from -0.125 to 0.125
- vectors: bfloat16 [2, 6144], P('section', 'fsdp'), may hold values from -2 to 2, as said below
- rel_table: float32 [2, 169, 16], P('section'), may hold values from -4 to 4
Outputs:
- layer_outputs: bfloat16 [2, 4, 16, 7, 14, 512], P('section', None, 'fsdp')
- input_grads: float32 [2, 4, 16, 7, 14, 512], P('section', None, 'fsdp')
- qkv_grad: float32 [2, 512, 1536], P('section', 'fsdp')
- proj_grad: float32 [2, 512, 512], P('section', 'fsdp')
- fc1_grad: float32 [2, 512, 2048], P('section', 'fsdp')
- fc2_grad: float32 [2, 2048, 512], P('section', 'fsdp')
- vectors_grad: float32 [2, 6144], P('section', 'fsdp')
- table_grad: float32 [2, 169, 16], P('section')
The draws below stay inside these ranges and needn't reach their ends.
Inputs may be any that keep to these rules, and one draw needn't show every extreme that they name: `vectors`: entries 0 to 511 and 2560 to 3071 of each row lie in 0.5 to 1.5.
All inputs are finite; a program needn't handle non-finite values.
Results may differ from the reference program's by a relative error of at most 0.015.
The reference program's roundings to bfloat16 on the way count: a program that leaves them out, or rounds other values in their place, can miss the bound.
Values may be sent and summed in bfloat16 or wider, within the bound.
A program may use at most 192 MiB of HBM per device.

```python
import jax
import jax.numpy as jnp
from jax import lax

D = 512
FF = 2048
H = 16
HD = 32
WIN = 7
SHIFT = 3
MB = 4
HALF_DEV = 1
SIDE = 14
TABLE_ROWS = 169
NV = 6144
GROUPS = 16
IMAGES = 8
N_FSDP = 16


def draw_vectors(key, part):
    first, second = jax.random.split(key)
    shape = (2, NV)
    index = jnp.arange(NV)
    gain_mask = (index < D) | (index >= 5 * D) & (index < 6 * D)
    gains = jax.random.uniform(first, shape, jnp.float32, 0.5, 1.5)
    biases = jnp.clip(0.5 * jax.random.normal(second, shape, jnp.float32), -2.0, 2.0)
    return jnp.where(gain_mask[None, :], gains, biases).astype(jnp.bfloat16)


def levels(rng, shape, cuts, smallest, largest):
    factor_of, own = 1.0, jax.random.fold_in(rng, 6)
    for dim, blocks in cuts:
        draws = jnp.exp(jax.random.uniform(jax.random.fold_in(own, dim), (blocks,), jnp.float32, smallest / len(cuts), largest / len(cuts)))
        factor_of = factor_of * jnp.repeat(draws, shape[dim] // blocks).reshape([-1 if axis == dim else 1 for axis in range(len(shape))])
    return factor_of


def scatter_about(key, dims, scale, reach, cuts=(), kind=jnp.bfloat16):
    entries = scale * jax.random.normal(key, dims, jnp.float32)
    if cuts:
        entries = entries * levels(key, dims, cuts, -0.22, 0.18)
    return jnp.clip(entries, -reach, reach).astype(kind)


def setup_inputs(seed: int = 0) -> dict:
    splits = jax.random.split(jax.random.key(seed), 9)
    block_input = scatter_about(splits[0], (MB, GROUPS, WIN, SIDE, D), 1.0, 6.0, ((1, 16),))
    cotangent = scatter_about(splits[1], (MB, GROUPS, WIN, SIDE, D), 1.0, 6.0, ((1, 16),))
    qkv_weight = scatter_about(splits[2], (2, D, 3 * D), D ** -0.5, 0.25, ((0, 2), (1, 16)))
    proj_weight = scatter_about(splits[3], (2, D, D), (D // (WIN * WIN)) ** -0.5, 2.0, ((0, 2), (1, 16)))
    fc1_weight = scatter_about(splits[4], (2, D, FF), D ** -0.5, 0.25, ((0, 2), (1, 16)))
    fc2_weight = scatter_about(splits[5], (2, FF, D), FF ** -0.5, 0.125, ((0, 2), (1, 16)))
    vectors = draw_vectors(jax.random.fold_in(splits[8], 71), 0)
    rel_table = scatter_about(splits[7], (2, TABLE_ROWS, H), 1.0, 4.0, ((0, 2),), jnp.float32)
    return dict(block_input=block_input, cotangent=cotangent, qkv_weight=qkv_weight, proj_weight=proj_weight, fc1_weight=fc1_weight, fc2_weight=fc2_weight, vectors=vectors, rel_table=rel_table)


EPS = 1e-05

def plain_product(first, second):
    return jnp.dot(first, second, preferred_element_type=jnp.float32)

def left_product(first, second):
    return lax.dot_general(first, second, (((0,), (0,)), ((), ())), preferred_element_type=jnp.float32)

def right_product(first, second):
    return lax.dot_general(first, second, (((1,), (1,)), ((), ())), preferred_element_type=jnp.float32)

def batched(form, first, second):
    return jnp.einsum(form, first.astype(jnp.float32), second.astype(jnp.float32))

def layer_norm(values, gain, offset):
    average = lax.optimization_barrier(jnp.mean(values, -1, keepdims=True))
    centred = values - average
    spread = lax.optimization_barrier(jnp.mean(centred * centred, -1, keepdims=True))
    return centred * lax.rsqrt(spread + EPS) * gain + offset

def to_windows(grid):
    batch, rows, cols, width = grid.shape
    grid = grid.reshape(batch, rows // WIN, WIN, cols // WIN, WIN, width)
    return grid.transpose(0, 1, 3, 2, 4, 5).reshape(-1, WIN * WIN, width)

def from_windows(tokens, batch, rows, cols):
    width = tokens.shape[-1]
    tokens = tokens.reshape(batch, rows // WIN, cols // WIN, WIN, WIN, width)
    return tokens.transpose(0, 1, 3, 2, 4, 5).reshape(batch, rows, cols, width)

def region(position):
    return (position >= SIDE - WIN).astype(jnp.int32) + (position >= SIDE - SHIFT).astype(jnp.int32)

def allowed_pairs(batch, row_start, rows, shifted_flag):
    row_index = row_start + jnp.arange(rows, dtype=jnp.int32)
    labels = region(row_index)[:, None] * 3 + region(jnp.arange(SIDE, dtype=jnp.int32))[None, :]
    labels = jnp.broadcast_to(labels[None, :, :, None], (batch, rows, SIDE, 1))
    windowed = to_windows(labels)[:, :, 0]
    same = windowed[:, :, None] == windowed[:, None, :]
    return same | jnp.logical_not(shifted_flag)

def relative_onehot():
    positions = jnp.arange(WIN * WIN, dtype=jnp.int32)
    prow = positions // WIN
    pcol = positions % WIN
    offset = (prow[:, None] - prow[None, :] + WIN - 1) * (2 * WIN - 1) + pcol[:, None] - pcol[None, :] + WIN - 1
    return (offset.reshape(-1)[:, None] == jnp.arange(TABLE_ROWS, dtype=jnp.int32)[None, :]).astype(jnp.float32)

def split_vectors(vector_row):
    values = vector_row.astype(jnp.float32)
    pieces = []
    start = 0
    for extent in [D] * 7 + [FF, D]:
        pieces.append(values[start:start + extent])
        start = start + extent
    return pieces

def recompute(grid_b, weights, vector_row, table, allowed, onehot):
    w_qkv, w_proj, w_up, w_down = weights
    parts = split_vectors(vector_row)
    base = to_windows(grid_b.astype(jnp.float32)).reshape(-1, D)
    normed = layer_norm(base, parts[0], parts[1]).astype(jnp.bfloat16)
    table_bias = jnp.dot(onehot, table, precision=lax.Precision.HIGHEST)
    table_bias = table_bias.reshape(WIN * WIN, WIN * WIN, H).transpose(2, 0, 1)
    mixed = plain_product(normed, w_qkv)
    scale = HD ** (-0.5)
    query = ((mixed[:, :D] + parts[2]) * scale).astype(jnp.bfloat16).reshape(-1, WIN * WIN, H, HD)
    keys = mixed[:, D:2 * D].astype(jnp.bfloat16).reshape(-1, WIN * WIN, H, HD)
    values = (mixed[:, 2 * D:] + parts[3]).astype(jnp.bfloat16).reshape(-1, WIN * WIN, H, HD)
    scores = batched('wihd,wjhd->whij', query, keys) + table_bias[None]
    scores = jnp.where(allowed[:, None], scores, -jnp.inf)
    highest = lax.optimization_barrier(jnp.max(scores, -1, keepdims=True))
    expo = jnp.exp(scores - highest)
    soft = expo / lax.optimization_barrier(jnp.sum(expo, -1, keepdims=True))
    attended = batched('whij,wjhd->wihd', soft.astype(jnp.bfloat16), values).astype(jnp.bfloat16).reshape(-1, D)
    middle = base + plain_product(attended, w_proj) + parts[4]
    second = layer_norm(middle, parts[5], parts[6]).astype(jnp.bfloat16)
    upward = plain_product(second, w_up) + parts[7]
    activated = jax.nn.gelu(upward, approximate=False).astype(jnp.bfloat16)
    result = middle + plain_product(activated, w_down) + parts[8]
    saved = (parts, base, normed, query, keys, values, soft, attended, middle, second, upward, activated)
    return (result, saved)

def block_forward(grid_b, weights, vector_row, table, allowed, onehot):
    batch, rows, cols, _ = grid_b.shape
    result, _ = recompute(grid_b, weights, vector_row, table, allowed, onehot)
    return from_windows(result.reshape(-1, WIN * WIN, D), batch, rows, cols)

def block_backward(grid_b, grad_grid, weights, vector_row, table, allowed, onehot):
    batch, rows, cols, _ = grid_b.shape
    w_qkv, w_proj, w_up, w_down = weights
    _, saved = recompute(grid_b, weights, vector_row, table, allowed, onehot)
    parts, base, normed, query, keys, values, soft, attended, middle, second, upward, activated = saved
    grad_out = to_windows(grad_grid).reshape(-1, D)
    down_in = grad_out.astype(jnp.bfloat16)
    grad_down = left_product(activated, down_in)
    grad_act = right_product(down_in, w_down)
    _, gelu_back = jax.vjp(lambda inner: jax.nn.gelu(inner, approximate=False), upward)
    grad_up = gelu_back(grad_act)[0]
    up_in = grad_up.astype(jnp.bfloat16)
    grad_upw = left_product(second, up_in)
    grad_second = right_product(up_in, w_up)
    _, second_back = jax.vjp(layer_norm, middle, parts[5], parts[6])
    grad_mid_norm, grad_gain2, grad_bias2 = second_back(grad_second)
    grad_mid = grad_out + grad_mid_norm
    proj_in = grad_mid.astype(jnp.bfloat16)
    grad_proj = left_product(attended, proj_in)
    grad_att = right_product(proj_in, w_proj).astype(jnp.bfloat16).reshape(-1, WIN * WIN, H, HD)
    grad_soft = batched('wihd,wjhd->whij', grad_att, values)
    grad_values = batched('whij,wihd->wjhd', soft.astype(jnp.bfloat16), grad_att)
    grad_scores = soft * (grad_soft - lax.optimization_barrier(jnp.sum(soft * grad_soft, -1, keepdims=True)))
    pair_sums = lax.optimization_barrier(jnp.sum(grad_scores, 0)).transpose(1, 2, 0).reshape(-1, grad_scores.shape[1])
    grad_table = lax.dot_general(onehot, pair_sums, (((0,), (0,)), ((), ())), precision=lax.Precision.HIGHEST)
    scores_b = grad_scores.astype(jnp.bfloat16)
    grad_query = (batched('whij,wjhd->wihd', scores_b, keys) * HD ** (-0.5)).reshape(-1, D)
    grad_keys = batched('whij,wihd->wjhd', scores_b, query).reshape(-1, D)
    grad_values = grad_values.reshape(-1, D)
    mixed_in = jnp.concatenate([grad_query, grad_keys, grad_values], 1).astype(jnp.bfloat16)
    grad_qkv = left_product(normed, mixed_in)
    grad_normed = right_product(mixed_in, w_qkv)
    _, first_back = jax.vjp(layer_norm, base, parts[0], parts[1])
    grad_base_norm, grad_gain1, grad_bias1 = first_back(grad_normed)
    grad_base = grad_mid + grad_base_norm
    grad_vectors = jnp.concatenate([grad_gain1, grad_bias1, lax.optimization_barrier(jnp.sum(grad_query, 0)), lax.optimization_barrier(jnp.sum(grad_values, 0)), lax.optimization_barrier(jnp.sum(grad_mid, 0)), grad_gain2, grad_bias2, lax.optimization_barrier(jnp.sum(grad_up, 0)), lax.optimization_barrier(jnp.sum(grad_out, 0))])
    grid_out = from_windows(grad_base.reshape(-1, WIN * WIN, D), batch, rows, cols)
    return (grid_out, (grad_qkv, grad_proj, grad_upw, grad_down, grad_vectors), grad_table)

def reference(block_input, cotangent, qkv_weight, proj_weight, fc1_weight, fc2_weight, vectors, rel_table):
    onehot = relative_onehot()

    def to_images(grouped):
        grouped = grouped.reshape(MB, N_FSDP // 2, 2, HALF_DEV, WIN, SIDE, D)
        return grouped.transpose(0, 1, 3, 2, 4, 5, 6).reshape(MB, IMAGES, SIDE, SIDE, D)

    def to_groups(images):
        images = images.reshape(MB, N_FSDP // 2, HALF_DEV, 2, WIN, SIDE, D)
        return images.transpose(0, 1, 3, 2, 4, 5, 6).reshape(MB, GROUPS, WIN, SIDE, D)

    def roll_in(grid):
        return jnp.roll(grid, (-SHIFT, -SHIFT), (1, 2))

    def roll_out(grid):
        return jnp.roll(grid, (SHIFT, SHIFT), (1, 2))
    plain_allowed = allowed_pairs(IMAGES, 0, SIDE, False)
    shift_allowed = allowed_pairs(IMAGES, 0, SIDE, True)
    first_weights = (qkv_weight[0], proj_weight[0], fc1_weight[0], fc2_weight[0])
    second_weights = (qkv_weight[1], proj_weight[1], fc1_weight[1], fc2_weight[1])

    def forward_first(images):
        return block_forward(images, first_weights, vectors[0], rel_table[0], plain_allowed, onehot).astype(jnp.bfloat16)

    def forward_second(images):
        result = block_forward(roll_in(images), second_weights, vectors[1], rel_table[1], shift_allowed, onehot)
        return roll_out(result.astype(jnp.bfloat16))
    inputs = to_images(block_input)
    first_out = lax.map(forward_first, inputs)
    second_out = lax.map(forward_second, first_out)

    def backward_second(pair):
        images, grad = pair
        grid, grads, table = block_backward(roll_in(images), roll_in(grad), second_weights, vectors[1], rel_table[1], shift_allowed, onehot)
        return (roll_out(grid), grads, table)

    def backward_first(pair):
        images, grad = pair
        return block_backward(images, grad, first_weights, vectors[0], rel_table[0], plain_allowed, onehot)
    second_back = lax.map(backward_second, (first_out, to_images(cotangent).astype(jnp.float32)))
    first_back = lax.map(backward_first, (inputs, second_back[0]))
    summed_second = jax.tree.map(lambda stacked: lax.optimization_barrier(jnp.sum(stacked, 0)), (second_back[1], second_back[2]))
    summed_first = jax.tree.map(lambda stacked: lax.optimization_barrier(jnp.sum(stacked, 0)), (first_back[1], first_back[2]))
    layer_outputs = jnp.stack([to_groups(first_out), to_groups(second_out)])
    input_grads = jnp.stack([to_groups(first_back[0]), to_groups(second_back[0])])
    grads = [jnp.stack([summed_first[0][index], summed_second[0][index]]) for index in range(5)]
    table_grad = jnp.stack([summed_first[1], summed_second[1]])
    return (layer_outputs, input_grads, grads[0], grads[1], grads[2], grads[3], grads[4], table_grad)
```

```python
import jax
import jax.numpy as jnp
from jax import lax
from jax.experimental import pallas as pl
from jax.experimental.pallas import tpu as pltpu
from jax.sharding import PartitionSpec as P

D = 512
FF = 2048
H = 16
HD = 32
WIN = 7
SHIFT = 3
SIDE = 14
TABLE_ROWS = 169


EPS = 1e-05


def partner(x, axis, apart):
    return lax.ppermute(x, axis, [(i, i ^ 1 << apart) for i in range(lax.axis_size(axis))])


def plain_product(first, second):
    return jnp.dot(first, second, preferred_element_type=jnp.float32)


def left_product(first, second):
    return lax.dot_general(
        first, second, (((0,), (0,)), ((), ())), preferred_element_type=jnp.float32
    )


def right_product(first, second):
    return lax.dot_general(
        first, second, (((1,), (1,)), ((), ())), preferred_element_type=jnp.float32
    )


def batched(form, first, second):
    return jnp.einsum(form, first, second, preferred_element_type=jnp.float32)


def layer_norm(values, gain, offset):
    average = jnp.mean(values, -1, keepdims=True)
    centred = values - average
    spread = jnp.mean(centred * centred, -1, keepdims=True)
    return centred * lax.rsqrt(spread + EPS) * gain + offset


def to_windows(grid):
    batch, rows, cols, width = grid.shape
    grid = grid.reshape(batch, rows // WIN, WIN, cols // WIN, WIN, width)
    return grid.transpose(0, 1, 3, 2, 4, 5).reshape(-1, WIN * WIN, width)


def from_windows(tokens, batch, rows, cols):
    width = tokens.shape[-1]
    tokens = tokens.reshape(batch, rows // WIN, cols // WIN, WIN, WIN, width)
    return tokens.transpose(0, 1, 3, 2, 4, 5).reshape(batch, rows, cols, width)


def region(position):
    return (position >= SIDE - WIN).astype(jnp.int32) + (position >= SIDE - SHIFT).astype(jnp.int32)


def allowed_pairs():
    index = jnp.arange(SIDE, dtype=jnp.int32)
    labels = region(index)[:, None] * 3 + region(index)[None, :]
    windowed = to_windows(labels[None, :, :, None])[:, :, 0]
    return windowed[:, :, None] == windowed[:, None, :]


def relative_onehot():
    positions = jnp.arange(WIN * WIN, dtype=jnp.int32)
    prow = positions // WIN
    pcol = positions % WIN
    offset = (
        (prow[:, None] - prow[None, :] + WIN - 1) * (2 * WIN - 1)
        + pcol[:, None]
        - pcol[None, :]
        + WIN
        - 1
    )
    return (offset.reshape(-1)[:, None] == jnp.arange(TABLE_ROWS, dtype=jnp.int32)[None, :]).astype(
        jnp.float32
    )


def split_vectors(vector_row):
    values = vector_row.astype(jnp.float32)
    pieces = []
    start = 0
    for extent in [D] * 7 + [FF, D]:
        pieces.append(values[start : start + extent])
        start = start + extent
    return pieces


def recompute(grid_b, weights, vector_row, table, allowed, onehot):
    w_qkv, w_proj, w_up, w_down = weights
    parts = split_vectors(vector_row)
    base = to_windows(grid_b.astype(jnp.float32)).reshape(-1, D)
    normed = layer_norm(base, parts[0], parts[1]).astype(jnp.bfloat16)
    table_bias = jnp.dot(onehot, table, precision=lax.Precision.HIGHEST)
    table_bias = table_bias.reshape(WIN * WIN, WIN * WIN, H).transpose(2, 0, 1)
    mixed = plain_product(normed, w_qkv)
    scale = HD ** (-0.5)
    query = ((mixed[:, :D] + parts[2]) * scale).astype(jnp.bfloat16).reshape(-1, WIN * WIN, H, HD)
    keys = mixed[:, D : 2 * D].astype(jnp.bfloat16).reshape(-1, WIN * WIN, H, HD)
    values = (mixed[:, 2 * D :] + parts[3]).astype(jnp.bfloat16).reshape(-1, WIN * WIN, H, HD)
    scores = batched("wihd,wjhd->whij", query, keys) + table_bias[None]
    if allowed is not None:
        windows = allowed.shape[0]
        scores = scores.reshape((-1, windows) + scores.shape[1:])
        scores = jnp.where(allowed[None, :, None], scores, -jnp.inf)
        scores = scores.reshape((-1,) + scores.shape[2:])
    highest = jnp.max(scores, -1, keepdims=True)
    expo = jnp.exp(scores - highest)
    soft = expo / jnp.sum(expo, -1, keepdims=True)
    attended = (
        batched("whij,wjhd->wihd", soft.astype(jnp.bfloat16), values)
        .astype(jnp.bfloat16)
        .reshape(-1, D)
    )
    middle = base + plain_product(attended, w_proj) + parts[4]
    second = layer_norm(middle, parts[5], parts[6]).astype(jnp.bfloat16)
    upward = plain_product(second, w_up) + parts[7]
    activated = jax.nn.gelu(upward, approximate=False).astype(jnp.bfloat16)
    result = middle + plain_product(activated, w_down) + parts[8]
    saved = (
        parts,
        base,
        normed,
        query,
        keys,
        values,
        soft,
        attended,
        middle,
        second,
        upward,
        activated,
    )
    return (result, saved)


def block_backward(saved, grad_grid, weights, onehot):
    batch, rows, cols, _ = grad_grid.shape
    w_qkv, w_proj, w_up, w_down = weights
    parts, base, normed, query, keys, values, soft, attended, middle, second, upward, activated = (
        saved
    )
    grad_out = to_windows(grad_grid).reshape(-1, D)
    down_in = grad_out.astype(jnp.bfloat16)
    grad_down = left_product(activated, down_in)
    grad_act = right_product(down_in, w_down)
    _, gelu_back = jax.vjp(lambda inner: jax.nn.gelu(inner, approximate=False), upward)
    grad_up = gelu_back(grad_act)[0]
    up_in = grad_up.astype(jnp.bfloat16)
    grad_upw = left_product(second, up_in)
    grad_second = right_product(up_in, w_up)
    _, second_back = jax.vjp(layer_norm, middle, parts[5], parts[6])
    grad_mid_norm, grad_gain2, grad_bias2 = second_back(grad_second)
    grad_mid = grad_out + grad_mid_norm
    proj_in = grad_mid.astype(jnp.bfloat16)
    grad_proj = left_product(attended, proj_in)
    grad_att = right_product(proj_in, w_proj).astype(jnp.bfloat16).reshape(-1, WIN * WIN, H, HD)
    grad_soft = batched("wihd,wjhd->whij", grad_att, values)
    grad_values = batched("whij,wihd->wjhd", soft.astype(jnp.bfloat16), grad_att)
    grad_scores = soft * (grad_soft - jnp.sum(soft * grad_soft, -1, keepdims=True))
    pair_sums = jnp.sum(grad_scores, 0).transpose(1, 2, 0).reshape(-1, grad_scores.shape[1])
    grad_table = lax.dot_general(
        onehot, pair_sums, (((0,), (0,)), ((), ())), precision=lax.Precision.HIGHEST
    )
    scores_b = grad_scores.astype(jnp.bfloat16)
    grad_query = (batched("whij,wjhd->wihd", scores_b, keys) * HD ** (-0.5)).reshape(-1, D)
    grad_keys = batched("whij,wihd->wjhd", scores_b, query).reshape(-1, D)
    grad_values = grad_values.reshape(-1, D)
    mixed_in = jnp.concatenate([grad_query, grad_keys, grad_values], 1).astype(jnp.bfloat16)
    grad_qkv = left_product(normed, mixed_in)
    grad_normed = right_product(mixed_in, w_qkv)
    _, first_back = jax.vjp(layer_norm, base, parts[0], parts[1])
    grad_base_norm, grad_gain1, grad_bias1 = first_back(grad_normed)
    grad_base = grad_mid + grad_base_norm
    grad_vectors = jnp.concatenate(
        [
            grad_gain1,
            grad_bias1,
            jnp.sum(grad_query, 0),
            jnp.sum(grad_values, 0),
            jnp.sum(grad_mid, 0),
            grad_gain2,
            grad_bias2,
            jnp.sum(grad_up, 0),
            jnp.sum(grad_out, 0),
        ]
    )
    grid_out = from_windows(grad_base.reshape(-1, WIN * WIN, D), batch, rows, cols)
    return (grid_out, (grad_qkv, grad_proj, grad_upw, grad_down, grad_vectors), grad_table)


MESH_IDS = pl.DeviceIdType.MESH


def ring_place(index, count):
    depth = count // 4
    layer = index // 4
    col = index % 4
    upper = col // 2
    rank = upper * 2 + (col % 2 + upper) % 2
    return rank * depth + layer + (rank % 2) * (depth - 1 - 2 * layer)


def ring_index(place, count):
    depth = count // 4
    place = (place + count) % count
    rank = place // depth
    rest = place % depth
    layer = rest + (rank % 2) * (depth - 1 - 2 * rest)
    upper = rank // 2
    return layer * 4 + upper * 2 + (rank % 2 + upper) % 2


def enter(section, me, ahead, behind):
    barrier = pltpu.get_barrier_semaphore()
    for target in ((section, ahead), (section, behind), (1 - section, me)):
        pl.semaphore_signal(barrier, inc=1, device_id=target, device_id_type=MESH_IDS)
    pl.semaphore_wait(barrier, 3)


def remote(src, dst, send, recv, target):
    return pltpu.make_async_remote_copy(
        src_ref=src,
        dst_ref=dst,
        send_sem=send,
        recv_sem=recv,
        device_id=target,
        device_id_type=MESH_IDS,
    )


def gather_kernel(count, own, whole, local_sem, up_s, up_r, down_s, down_r, side_s, side_r):
    section = lax.axis_index("section")
    me = lax.axis_index("fsdp")
    place = ring_place(me, count)
    ahead = ring_index(place + 1, count)
    behind = ring_index(place - 1, count)
    ups = count // 2
    downs = count - 1 - ups
    keep = pltpu.make_async_copy(own, whole.at[section, me], local_sem)
    keep.start()
    enter(section, me, ahead, behind)
    sides = []

    def up_copy(step):
        block = ring_index(place - step, count)
        piece = own if step == 0 else whole.at[section, block]
        return remote(
            piece, whole.at[section, block], up_s.at[step], up_r.at[step], (section, ahead)
        )

    def down_copy(step):
        block = ring_index(place + step, count)
        piece = own if step == 0 else whole.at[section, block]
        return remote(
            piece, whole.at[section, block], down_s.at[step], down_r.at[step], (section, behind)
        )

    def side_copy(block, piece, slot):
        return remote(
            piece, whole.at[section, block], side_s.at[slot], side_r.at[slot], (1 - section, me)
        )

    going = []
    for step in range(ups):
        up = up_copy(step)
        up.start()
        going.append(up)
        if step < downs:
            down = down_copy(step)
            down.start()
            going.append(down)
        if step == 0:
            side = side_copy(me, own, 0)
            side.start()
            sides.append(side)
        up.wait_recv()
        block = ring_index(place - step - 1, count)
        side = side_copy(block, whole.at[section, block], 1 + step)
        side.start()
        sides.append(side)
        if step < downs:
            down.wait_recv()
            block = ring_index(place + step + 1, count)
            side = side_copy(block, whole.at[section, block], 1 + ups + step)
            side.start()
            sides.append(side)
    for copy in going:
        copy.wait_send()
    for copy in sides:
        copy.wait()
    keep.wait()


def gather_all(own, sections, count):
    ups = count // 2
    return pl.pallas_call(
        lambda *refs: gather_kernel(count, *refs),
        out_shape=jax.ShapeDtypeStruct((sections, count) + own.shape, own.dtype),
        in_specs=[pl.BlockSpec(memory_space=pl.ANY)],
        out_specs=pl.BlockSpec(memory_space=pl.ANY),
        scratch_shapes=[
            pltpu.SemaphoreType.DMA,
            pltpu.SemaphoreType.DMA((ups,)),
            pltpu.SemaphoreType.DMA((ups,)),
            pltpu.SemaphoreType.DMA((ups,)),
            pltpu.SemaphoreType.DMA((ups,)),
            pltpu.SemaphoreType.DMA((count,)),
            pltpu.SemaphoreType.DMA((count,)),
        ],
        compiler_params=pltpu.CompilerParams(collective_id=0, has_side_effects=True),
        name="gather_weights",
    )(own)


def scatter_kernel(
    count,
    parts,
    out,
    mine,
    theirs,
    first,
    up_buf,
    down_buf,
    local_sem,
    up_s,
    up_r,
    down_s,
    down_r,
    side_s,
    side_r,
):
    section = lax.axis_index("section")
    me = lax.axis_index("fsdp")
    place = ring_place(me, count)
    ahead = ring_index(place + 1, count)
    behind = ring_index(place - 1, count)
    ups = count // 2
    downs = count - 1 - ups
    keep = pltpu.make_async_copy(parts.at[section], mine, local_sem)
    keep.start()
    enter(section, me, ahead, behind)
    offsets = []
    for step in range(ups):
        offsets.append(ups - step)
        if step < downs:
            offsets.append(step - downs)
    offsets.append(0)
    sides = {}
    for slot, offset in enumerate(offsets):
        block = ring_index(place + offset, count)
        side = remote(
            parts.at[1 - section, block],
            theirs.at[block],
            side_s.at[slot],
            side_r.at[slot],
            (1 - section, me),
        )
        side.start()
        sides[offset] = side
    keep.wait()

    def local(offset):
        sides[offset].wait_recv()
        block = ring_index(place + offset, count)
        return mine[block].astype(jnp.float32) + theirs[block].astype(jnp.float32)

    ups_sent = []
    downs_sent = []
    for step in range(ups):
        value = local(ups - step)
        if step == 0:
            held = first.at[0]
        else:
            ups_sent[-1].wait_recv()
            held = up_buf.at[step - 1]
            value = value + held[...].astype(jnp.float32)
        held[...] = value.astype(held.dtype)
        copy = remote(held, up_buf.at[step], up_s.at[step], up_r.at[step], (section, ahead))
        copy.start()
        ups_sent.append(copy)
        if step < downs:
            value = local(step - downs)
            if step == 0:
                held = first.at[1]
            else:
                downs_sent[-1].wait_recv()
                held = down_buf.at[step - 1]
                value = value + held[...].astype(jnp.float32)
            held[...] = value.astype(held.dtype)
            copy = remote(
                held, down_buf.at[step], down_s.at[step], down_r.at[step], (section, behind)
            )
            copy.start()
            downs_sent.append(copy)
    value = local(0)
    ups_sent[-1].wait_recv()
    value = value + up_buf[ups - 1].astype(jnp.float32)
    downs_sent[-1].wait_recv()
    out[...] = value + down_buf[downs - 1].astype(jnp.float32)
    for copy in ups_sent + downs_sent:
        copy.wait_send()
    for side in sides.values():
        side.wait_send()


def scatter_all(parts, count):
    ups = count // 2
    downs = count - 1 - ups
    block = parts.shape[2:]
    kind = parts.dtype
    return pl.pallas_call(
        lambda *refs: scatter_kernel(count, *refs),
        out_shape=jax.ShapeDtypeStruct(block, jnp.float32),
        in_specs=[pl.BlockSpec(memory_space=pl.ANY)],
        out_specs=pl.BlockSpec(memory_space=pltpu.VMEM),
        scratch_shapes=[
            pltpu.VMEM((count,) + block, kind),
            pltpu.VMEM((count,) + block, kind),
            pltpu.VMEM((2,) + block, kind),
            pltpu.VMEM((ups,) + block, kind),
            pltpu.VMEM((downs,) + block, kind),
            pltpu.SemaphoreType.DMA,
            pltpu.SemaphoreType.DMA((ups,)),
            pltpu.SemaphoreType.DMA((ups,)),
            pltpu.SemaphoreType.DMA((ups,)),
            pltpu.SemaphoreType.DMA((ups,)),
            pltpu.SemaphoreType.DMA((count,)),
            pltpu.SemaphoreType.DMA((count,)),
        ],
        compiler_params=pltpu.CompilerParams(collective_id=1, has_side_effects=True),
        name="scatter_grads",
    )(parts)


EXTRA = 16


def pack(qkv, proj, up, down, row):
    owners = qkv.shape[0]
    pieces = []
    for matrix in (qkv, proj, up, down):
        for start in range(0, matrix.shape[2], D):
            pieces.append(matrix[:, :, start : start + D])
    row = jnp.pad(row[:, None, :], ((0, 0), (0, EXTRA - 1), (0, D - row.shape[1])))
    return jnp.concatenate(pieces + [row], 1).reshape(owners, -1, D)


def unpack(packed, share, down_share, width):
    start = 0
    matrices = []
    for extent, rows in ((3 * D, share), (D, share), (FF, share), (D, down_share)):
        pieces = []
        for _ in range(extent // D):
            pieces.append(packed[:, start : start + rows])
            start = start + rows
        matrices.append(jnp.concatenate(pieces, 2).reshape(-1, extent))
    return matrices, packed[:, start, :width].reshape(-1)


def by_flag(flag, first, second):
    return jnp.where(flag == 0, jnp.stack([first, second]), jnp.stack([second, first]))


def swap_sections(value):
    return lax.ppermute(value, "section", [(0, 1), (1, 0)])


def whole_images(halves, section, half):
    share = halves.shape[1] // (2 * lax.axis_size("section"))
    own = lax.dynamic_slice_in_dim(halves, (section * 2 + half) * share, share, 1)
    away = lax.dynamic_slice_in_dim(halves, (section * 2 + 1 - half) * share, share, 1)
    both = by_flag(half, own, partner(away, "fsdp", 0))
    both = both.transpose(1, 2, 3, 0, 4, 5, 6)
    return both.reshape(both.shape[0], -1, SIDE, SIDE, D)


def spread_images(first, second, section, half, groups):
    mine = jnp.where(section == 0, first, second)
    other = jnp.where(section == 0, second, first)
    both = by_flag(section, mine, swap_sections(other))
    both = both.reshape(both.shape[0], -1, groups, 2, WIN, SIDE, D)
    kept = jnp.where(half == 0, both[:, :, :, 0], both[:, :, :, 1])
    away = jnp.where(half == 0, both[:, :, :, 1], both[:, :, :, 0])
    halves = by_flag(half, kept, partner(away, "fsdp", 0))
    return halves.transpose(1, 0, 2, 3, 4, 5, 6).reshape(-1, groups, WIN, SIDE, D)


def on_device(
    block_input, cotangent, qkv_weight, proj_weight, fc1_weight, fc2_weight, vectors, rel_table
):
    section = lax.axis_index("section")
    sections = lax.axis_size("section")
    half = lax.axis_index("fsdp") % 2
    count = lax.axis_size("fsdp")
    groups = block_input.shape[1]
    share = qkv_weight.shape[1]
    down_share = fc2_weight.shape[1]
    width = vectors.shape[1]
    onehot = relative_onehot()
    gathered = gather_all(
        pack(qkv_weight, proj_weight, fc1_weight, fc2_weight, vectors)[0], sections, count
    )
    images = whole_images(jnp.stack([block_input, cotangent]), section, half)
    tables = by_flag(section, rel_table[0], swap_sections(rel_table[0]))
    layers = [unpack(gathered[layer], share, down_share, width) for layer in range(2)]
    masks = (None, allowed_pairs())

    def forward(grid, layer):
        weights, row = layers[layer]
        result, saved = recompute(grid, weights, row, tables[layer], masks[layer], onehot)
        batch = grid.shape[0]
        out = from_windows(result.reshape(-1, WIN * WIN, D).astype(jnp.bfloat16), batch, SIDE, SIDE)
        return out, saved

    first_out, first_saved = forward(images[0], 0)
    second_out, second_saved = forward(jnp.roll(first_out, (-SHIFT, -SHIFT), (1, 2)), 1)
    second_out = jnp.roll(second_out, (SHIFT, SHIFT), (1, 2))
    grad = jnp.roll(images[1], (-SHIFT, -SHIFT), (1, 2)).astype(jnp.float32)
    second_grid, second_grads, second_table = block_backward(
        second_saved, grad, layers[1][0], onehot
    )
    second_grid = jnp.roll(second_grid, (SHIFT, SHIFT), (1, 2))
    first_grid, first_grads, first_table = block_backward(
        first_saved, second_grid, layers[0][0], onehot
    )

    def owners(grads):
        shaped = [piece.reshape(count, -1, piece.shape[-1]) for piece in grads[:4]]
        return pack(*shaped, grads[4].reshape(count, -1)).astype(jnp.bfloat16)

    summed = scatter_all(jnp.stack([owners(first_grads), owners(second_grads)]), count)
    mine, row = unpack(summed[None], share, down_share, width)
    table_total = lax.psum(jnp.stack([first_table, second_table]), ("section", "fsdp"))
    table_total = jnp.where(section == 0, table_total[0], table_total[1])
    produced = spread_images(first_out, second_out, section, half, groups)
    returned = spread_images(
        first_grid.astype(jnp.bfloat16), second_grid.astype(jnp.bfloat16), section, half, groups
    ).astype(jnp.float32)
    return (
        produced[None],
        returned[None],
        mine[0][None],
        mine[1][None],
        mine[2][None],
        mine[3][None],
        row[None],
        table_total[None],
    )


def solution(mesh):
    in_specs = (
        P(None, "fsdp", None, None, None),
        P(None, "fsdp", None, None, None),
        P("section", "fsdp", None),
        P("section", "fsdp", None),
        P("section", "fsdp", None),
        P("section", "fsdp", None),
        P("section", "fsdp"),
        P("section", None, None),
    )
    out_specs = (
        P("section", None, "fsdp", None, None, None),
        P("section", None, "fsdp", None, None, None),
        P("section", "fsdp", None),
        P("section", "fsdp", None),
        P("section", "fsdp", None),
        P("section", "fsdp", None),
        P("section", "fsdp"),
        P("section", None, None),
    )
    return jax.shard_map(
        on_device, mesh=mesh, in_specs=in_specs, out_specs=out_specs, check_vma=False
    )
```

```python
import jax
import jax.numpy as jnp
from jax import lax
from jax.experimental import pallas as pl
from jax.experimental.pallas import tpu as pltpu
from jax.sharding import PartitionSpec as P

D = 512
FF = 2048
H = 16
HD = 32
WIN = 7
SHIFT = 3
SIDE = 14
TABLE_ROWS = 169


EPS = 1e-05


def partner(x, axis, apart):
    return lax.ppermute(x, axis, [(i, i ^ 1 << apart) for i in range(lax.axis_size(axis))])


def plain_product(first, second):
    return jnp.dot(first, second, preferred_element_type=jnp.float32)


def left_product(first, second):
    return lax.dot_general(
        first, second, (((0,), (0,)), ((), ())), preferred_element_type=jnp.float32
    )


def right_product(first, second):
    return lax.dot_general(
        first, second, (((1,), (1,)), ((), ())), preferred_element_type=jnp.float32
    )


def to_windows(grid):
    batch, rows, cols, width = grid.shape
    grid = grid.reshape(batch, rows // WIN, WIN, cols // WIN, WIN, width)
    return grid.transpose(0, 1, 3, 2, 4, 5).reshape(-1, WIN * WIN, width)


def from_windows(tokens, batch, rows, cols):
    width = tokens.shape[-1]
    tokens = tokens.reshape(batch, rows // WIN, cols // WIN, WIN, WIN, width)
    return tokens.transpose(0, 1, 3, 2, 4, 5).reshape(batch, rows, cols, width)


def region(position):
    return (position >= SIDE - WIN).astype(jnp.int32) + (position >= SIDE - SHIFT).astype(jnp.int32)


def allowed_pairs():
    index = jnp.arange(SIDE, dtype=jnp.int32)
    labels = region(index)[:, None] * 3 + region(index)[None, :]
    windowed = to_windows(labels[None, :, :, None])[:, :, 0]
    return windowed[:, :, None] == windowed[:, None, :]


def relative_onehot():
    positions = jnp.arange(WIN * WIN, dtype=jnp.int32)
    prow = positions // WIN
    pcol = positions % WIN
    offset = (
        (prow[:, None] - prow[None, :] + WIN - 1) * (2 * WIN - 1)
        + pcol[:, None]
        - pcol[None, :]
        + WIN
        - 1
    )
    return (offset.reshape(-1)[:, None] == jnp.arange(TABLE_ROWS, dtype=jnp.int32)[None, :]).astype(
        jnp.float32
    )


PADDED = 64
LANES = 128
BLOCKS = 12
FAR = -1e30


def normalise(values):
    centred = values - jnp.mean(values, -1, keepdims=True)
    inverse = lax.rsqrt(jnp.mean(centred * centred, -1, keepdims=True) + EPS)
    return centred * inverse, inverse


def normalise_back(scaled, inverse, gain, grad):
    inner = grad * gain
    first = jnp.mean(inner, -1, keepdims=True)
    second = jnp.mean(inner * scaled, -1, keepdims=True)
    return inverse * (inner - first - scaled * second)


def block_of(ref, index):
    owners, rows, _ = ref.shape
    share = D // owners
    if index < 8:
        return (slice(None), slice(index * share, (index + 1) * share))
    part = index - 8
    if owners == 1:
        return (slice(None), slice(index * D, (index + 1) * D))
    quarter = owners // 4
    return (slice(part * quarter, (part + 1) * quarter), slice(8 * share, 12 * share))


def weight(ref, index):
    return ref[block_of(ref, index)].reshape(D, D)


def put(ref, index, value):
    place = block_of(ref, index)
    shape = ref[place].shape
    ref[place] = value.astype(ref.dtype).reshape(shape)


def head_lanes(head):
    lane = lax.broadcasted_iota(jnp.int32, (1, LANES), 1)
    return lane // HD == head


def spread_heads(piece):
    zero = jnp.zeros_like(piece)
    return jnp.concatenate([jnp.where(head_lanes(h), piece, zero) for h in range(LANES // HD)], 0)


def join_heads(tall):
    rows = tall.shape[0] // (LANES // HD)
    total = jnp.where(head_lanes(0), tall[:rows], 0.0)
    for h in range(1, LANES // HD):
        total = total + jnp.where(head_lanes(h), tall[h * rows : (h + 1) * rows], 0.0)
    return total


def cols(index, width=D):
    return slice(index * width, (index + 1) * width)


def forward_kernel(x, w, vec, bias, out, normed, mixed, soft, att, mid, second, up, act):
    base = x[...].astype(jnp.float32)
    scaled, _ = normalise(base)
    normed[...] = (scaled * vec[0:1] + vec[1:2]).astype(jnp.bfloat16)
    query = plain_product(normed[...], weight(w, 0))
    mixed[:, cols(0)] = ((query + vec[2:3]) * HD ** (-0.5)).astype(jnp.bfloat16)
    mixed[:, cols(1)] = plain_product(normed[...], weight(w, 1)).astype(jnp.bfloat16)
    values = plain_product(normed[...], weight(w, 2))
    mixed[:, cols(2)] = (values + vec[3:4]).astype(jnp.bfloat16)
    groups = D // LANES
    for window in range(x.shape[0] // PADDED):
        rows = cols(window, PADDED)
        for group in range(groups):
            q = spread_heads(mixed[rows, cols(group, LANES)])
            k = mixed[rows, cols(groups + group, LANES)]
            v = mixed[rows, cols(2 * groups + group, LANES)]
            scores = right_product(q, k) + bias[window % bias.shape[0], group]
            expo = jnp.exp(scores - jnp.max(scores, -1, keepdims=True))
            prob = expo / jnp.sum(expo, -1, keepdims=True)
            soft[window * groups + group] = prob
            tall = plain_product(prob.astype(jnp.bfloat16), v)
            att[rows, cols(group, LANES)] = join_heads(tall).astype(jnp.bfloat16)
    middle = base + plain_product(att[...], weight(w, 3)) + vec[4:5]
    mid[...] = middle
    scaled, _ = normalise(middle)
    second[...] = (scaled * vec[5:6] + vec[6:7]).astype(jnp.bfloat16)
    total = middle + vec[11:12]
    for part in range(FF // D):
        upward = plain_product(second[...], weight(w, 4 + part)) + vec[7 + part : 8 + part]
        up[:, cols(part)] = upward
        activated = (0.5 * upward * (1.0 + lax.erf(upward * 0.5**0.5))).astype(jnp.bfloat16)
        act[:, cols(part)] = activated
        total = total + plain_product(activated, weight(w, 8 + part))
    out[...] = total.astype(jnp.bfloat16)


def backward_kernel(
    grad, x, w, vec, normed, mixed, soft, att, mid, second, up, act, dx, dw, dvec, dscore, datt, dmix
):
    grad_out = grad[...]
    down_in = grad_out.astype(jnp.bfloat16)
    grad_second = jnp.zeros(grad_out.shape, jnp.float32)
    for part in range(FF // D):
        grad_act = right_product(down_in, weight(w, 8 + part))
        upward = up[:, cols(part)]
        slope = 0.5 * (1.0 + lax.erf(upward * 0.5**0.5))
        slope = slope + upward * jnp.exp(-0.5 * upward * upward) * 0.3989422804014327
        grad_up = grad_act * slope
        dvec[7 + part : 8 + part] = jnp.sum(grad_up, 0, keepdims=True)
        up_in = grad_up.astype(jnp.bfloat16)
        put(dw, 4 + part, left_product(second[...], up_in))
        put(dw, 8 + part, left_product(act[:, cols(part)], down_in))
        grad_second = grad_second + right_product(up_in, weight(w, 4 + part))
    dvec[11:12] = jnp.sum(grad_out, 0, keepdims=True)
    scaled, inverse = normalise(mid[...])
    dvec[5:6] = jnp.sum(grad_second * scaled, 0, keepdims=True)
    dvec[6:7] = jnp.sum(grad_second, 0, keepdims=True)
    grad_mid = grad_out + normalise_back(scaled, inverse, vec[5:6], grad_second)
    dvec[4:5] = jnp.sum(grad_mid, 0, keepdims=True)
    proj_in = grad_mid.astype(jnp.bfloat16)
    put(dw, 3, left_product(att[...], proj_in))
    datt[...] = right_product(proj_in, weight(w, 3)).astype(jnp.bfloat16)
    groups = D // LANES
    for group in range(groups):
        lanes = cols(group, LANES)
        scores_sum = jnp.zeros(dscore.shape[1:], jnp.float32)
        query_sum = jnp.zeros((1, LANES), jnp.float32)
        value_sum = jnp.zeros((1, LANES), jnp.float32)
        for window in range(x.shape[0] // PADDED):
            rows = cols(window, PADDED)
            q = spread_heads(mixed[rows, lanes])
            k = mixed[rows, cols(groups + group, LANES)]
            v = mixed[rows, cols(2 * groups + group, LANES)]
            prob = soft[window * groups + group]
            away = spread_heads(datt[rows, lanes])
            grad_soft = right_product(away, v)
            grad_values = left_product(prob.astype(jnp.bfloat16), away)
            total = jnp.sum(prob * grad_soft, -1, keepdims=True)
            grad_scores = prob * (grad_soft - total)
            scores_sum = scores_sum + grad_scores
            scores_b = grad_scores.astype(jnp.bfloat16)
            grad_query = join_heads(plain_product(scores_b, k)) * HD ** (-0.5)
            grad_keys = left_product(scores_b, q)
            query_sum = query_sum + jnp.sum(grad_query, 0, keepdims=True)
            value_sum = value_sum + jnp.sum(grad_values, 0, keepdims=True)
            dmix[rows, lanes] = grad_query.astype(jnp.bfloat16)
            dmix[rows, cols(groups + group, LANES)] = grad_keys.astype(jnp.bfloat16)
            dmix[rows, cols(2 * groups + group, LANES)] = grad_values.astype(jnp.bfloat16)
        dscore[group] = scores_sum
        dvec[2:3, lanes] = query_sum
        dvec[3:4, lanes] = value_sum
    grad_normed = jnp.zeros(grad_out.shape, jnp.float32)
    for part in range(3):
        piece = dmix[:, cols(part)]
        put(dw, part, left_product(normed[...], piece))
        grad_normed = grad_normed + right_product(piece, weight(w, part))
    scaled, inverse = normalise(x[...].astype(jnp.float32))
    dvec[0:1] = jnp.sum(grad_normed * scaled, 0, keepdims=True)
    dvec[1:2] = jnp.sum(grad_normed, 0, keepdims=True)
    dx[...] = grad_mid + normalise_back(scaled, inverse, vec[0:1], grad_normed)


def in_vmem(count):
    return [pl.BlockSpec(memory_space=pltpu.VMEM)] * count


def shaped(kind, *shape):
    return jax.ShapeDtypeStruct(shape, kind)


def run_forward(x, w, vec, bias):
    rows = x.shape[0]
    half, full = jnp.bfloat16, jnp.float32
    units = rows // PADDED * (D // LANES)
    shapes = (
        shaped(half, rows, D),
        shaped(half, rows, D),
        shaped(half, rows, 3 * D),
        shaped(full, units, PADDED * LANES // HD, PADDED),
        shaped(half, rows, D),
        shaped(full, rows, D),
        shaped(half, rows, D),
        shaped(full, rows, FF),
        shaped(half, rows, FF),
    )
    return pl.pallas_call(
        forward_kernel,
        out_shape=shapes,
        in_specs=in_vmem(4),
        out_specs=tuple(in_vmem(len(shapes))),
        compiler_params=pltpu.CompilerParams(vmem_limit_bytes=56 << 20),
        name="layer_forward",
    )(x, w, vec, bias)


def run_backward(grad, x, w, vec, saved):
    rows = x.shape[0]
    half, full = jnp.bfloat16, jnp.float32
    shapes = (
        shaped(full, rows, D),
        shaped(half, w.shape[0], BLOCKS * D // w.shape[0], D),
        shaped(full, BLOCKS, D),
        shaped(full, D // LANES, PADDED * LANES // HD, PADDED),
    )
    return pl.pallas_call(
        backward_kernel,
        out_shape=shapes,
        in_specs=in_vmem(4 + len(saved)),
        out_specs=tuple(in_vmem(len(shapes))),
        scratch_shapes=[pltpu.VMEM((rows, D), half), pltpu.VMEM((rows, 3 * D), half)],
        compiler_params=pltpu.CompilerParams(vmem_limit_bytes=56 << 20),
        name="layer_backward",
    )(grad, x, w, vec, *saved)


def pad_windows(grid):
    tokens = to_windows(grid)
    return jnp.pad(tokens, ((0, 0), (0, PADDED - WIN * WIN), (0, 0))).reshape(-1, D)


def unpad_windows(rows, batch):
    return from_windows(rows.reshape(-1, PADDED, D)[:, : WIN * WIN], batch, SIDE, SIDE)


def score_bias(table, allowed, onehot):
    bias = jnp.dot(onehot, table, precision=lax.Precision.HIGHEST)
    bias = bias.reshape(WIN * WIN, WIN * WIN, H).transpose(2, 0, 1)[None]
    if allowed is not None:
        bias = jnp.where(allowed[:, None], bias, FAR)
    short = PADDED - WIN * WIN
    bias = jnp.pad(bias, ((0, 0), (0, 0), (0, short), (0, 0)))
    bias = jnp.pad(bias, ((0, 0), (0, 0), (0, 0), (0, short)), constant_values=FAR)
    return bias.reshape(bias.shape[0], D // LANES, -1, PADDED)


def table_sums(dscore, onehot):
    sums = dscore.reshape(H, PADDED, PADDED)[:, : WIN * WIN, : WIN * WIN]
    sums = sums.transpose(1, 2, 0).reshape(-1, H)
    return lax.dot_general(
        onehot, sums, (((0,), (0,)), ((), ())), precision=lax.Precision.HIGHEST
    )


def regroup(packed, share):
    if share % 16 == 0:
        return packed
    owners = packed.shape[0]
    pieces = [packed[:, cols(c, share)].reshape(1, D, D) for c in range(8)]
    pieces.append(packed[:, 8 * share : 12 * share].reshape(1, FF, D))
    return jnp.concatenate(pieces, 1)


def ungroup(whole, owners):
    if whole.shape[0] == owners:
        return whole
    pieces = [whole[0, cols(c)].reshape(owners, -1, D) for c in range(8)]
    pieces.append(whole[0, 8 * D :].reshape(owners, -1, D))
    return jnp.concatenate(pieces, 1)


MESH_IDS = pl.DeviceIdType.MESH


def ring_place(index, count):
    depth = count // 4
    layer = index // 4
    col = index % 4
    upper = col // 2
    rank = upper * 2 + (col % 2 + upper) % 2
    return rank * depth + layer + (rank % 2) * (depth - 1 - 2 * layer)


def ring_index(place, count):
    depth = count // 4
    place = (place + count) % count
    rank = place // depth
    rest = place % depth
    layer = rest + (rank % 2) * (depth - 1 - 2 * rest)
    upper = rank // 2
    return layer * 4 + upper * 2 + (rank % 2 + upper) % 2


def enter(section, me, ahead, behind):
    barrier = pltpu.get_barrier_semaphore()
    for target in ((section, ahead), (section, behind), (1 - section, me)):
        pl.semaphore_signal(barrier, inc=1, device_id=target, device_id_type=MESH_IDS)
    pl.semaphore_wait(barrier, 3)


def remote(src, dst, send, recv, target):
    return pltpu.make_async_remote_copy(
        src_ref=src,
        dst_ref=dst,
        send_sem=send,
        recv_sem=recv,
        device_id=target,
        device_id_type=MESH_IDS,
    )


def gather_kernel(count, own, whole, local_sem, up_s, up_r, down_s, down_r, side_s, side_r):
    section = lax.axis_index("section")
    me = lax.axis_index("fsdp")
    place = ring_place(me, count)
    ahead = ring_index(place + 1, count)
    behind = ring_index(place - 1, count)
    ups = count // 2
    downs = count - 1 - ups
    keep = pltpu.make_async_copy(own, whole.at[section, me], local_sem)
    keep.start()
    enter(section, me, ahead, behind)
    sides = []

    def up_copy(step):
        block = ring_index(place - step, count)
        piece = own if step == 0 else whole.at[section, block]
        return remote(
            piece, whole.at[section, block], up_s.at[step], up_r.at[step], (section, ahead)
        )

    def down_copy(step):
        block = ring_index(place + step, count)
        piece = own if step == 0 else whole.at[section, block]
        return remote(
            piece, whole.at[section, block], down_s.at[step], down_r.at[step], (section, behind)
        )

    def side_copy(block, piece, slot):
        return remote(
            piece, whole.at[section, block], side_s.at[slot], side_r.at[slot], (1 - section, me)
        )

    going = []
    for step in range(ups):
        up = up_copy(step)
        up.start()
        going.append(up)
        if step < downs:
            down = down_copy(step)
            down.start()
            going.append(down)
        if step == 0:
            side = side_copy(me, own, 0)
            side.start()
            sides.append(side)
        up.wait_recv()
        block = ring_index(place - step - 1, count)
        side = side_copy(block, whole.at[section, block], 1 + step)
        side.start()
        sides.append(side)
        if step < downs:
            down.wait_recv()
            block = ring_index(place + step + 1, count)
            side = side_copy(block, whole.at[section, block], 1 + ups + step)
            side.start()
            sides.append(side)
    for copy in going:
        copy.wait_send()
    for copy in sides:
        copy.wait()
    keep.wait()


def gather_all(own, sections, count):
    ups = count // 2
    return pl.pallas_call(
        lambda *refs: gather_kernel(count, *refs),
        out_shape=jax.ShapeDtypeStruct((sections, count) + own.shape, own.dtype),
        in_specs=[pl.BlockSpec(memory_space=pl.ANY)],
        out_specs=pl.BlockSpec(memory_space=pl.ANY),
        scratch_shapes=[
            pltpu.SemaphoreType.DMA,
            pltpu.SemaphoreType.DMA((ups,)),
            pltpu.SemaphoreType.DMA((ups,)),
            pltpu.SemaphoreType.DMA((ups,)),
            pltpu.SemaphoreType.DMA((ups,)),
            pltpu.SemaphoreType.DMA((count,)),
            pltpu.SemaphoreType.DMA((count,)),
        ],
        compiler_params=pltpu.CompilerParams(collective_id=0, has_side_effects=True),
        name="gather_weights",
    )(own)


def scatter_kernel(
    count,
    part0,
    part1,
    out,
    mine,
    theirs,
    first,
    up_buf,
    down_buf,
    local_sem,
    up_s,
    up_r,
    down_s,
    down_r,
    side_s,
    side_r,
):
    section = lax.axis_index("section")
    me = lax.axis_index("fsdp")
    place = ring_place(me, count)
    ahead = ring_index(place + 1, count)
    behind = ring_index(place - 1, count)
    ups = count // 2
    downs = count - 1 - ups
    keep = [pltpu.make_async_copy(part, mine, local_sem) for part in (part0, part1)]
    pl.when(section == 0)(keep[0].start)
    pl.when(section == 1)(keep[1].start)
    enter(section, me, ahead, behind)
    offsets = []
    for step in range(ups):
        offsets.append(ups - step)
        if step < downs:
            offsets.append(step - downs)
    offsets.append(0)
    sides = {}
    for slot, offset in enumerate(offsets):
        block = ring_index(place + offset, count)
        pair = [
            remote(
                part.at[block],
                theirs.at[block],
                side_s.at[slot],
                side_r.at[slot],
                (1 - section, me),
            )
            for part in (part0, part1)
        ]
        pl.when(section == 0)(pair[1].start)
        pl.when(section == 1)(pair[0].start)
        sides[offset] = pair[0]
    keep[0].wait()

    def local(offset):
        sides[offset].wait_recv()
        block = ring_index(place + offset, count)
        return mine[block].astype(jnp.float32) + theirs[block].astype(jnp.float32)

    ups_sent = []
    downs_sent = []
    for step in range(ups):
        value = local(ups - step)
        if step == 0:
            held = first.at[0]
        else:
            ups_sent[-1].wait_recv()
            held = up_buf.at[step - 1]
            value = value + held[...].astype(jnp.float32)
        held[...] = value.astype(held.dtype)
        copy = remote(held, up_buf.at[step], up_s.at[step], up_r.at[step], (section, ahead))
        copy.start()
        ups_sent.append(copy)
        if step < downs:
            value = local(step - downs)
            if step == 0:
                held = first.at[1]
            else:
                downs_sent[-1].wait_recv()
                held = down_buf.at[step - 1]
                value = value + held[...].astype(jnp.float32)
            held[...] = value.astype(held.dtype)
            copy = remote(
                held, down_buf.at[step], down_s.at[step], down_r.at[step], (section, behind)
            )
            copy.start()
            downs_sent.append(copy)
    value = local(0)
    ups_sent[-1].wait_recv()
    value = value + up_buf[ups - 1].astype(jnp.float32)
    downs_sent[-1].wait_recv()
    out[...] = value + down_buf[downs - 1].astype(jnp.float32)
    for copy in ups_sent + downs_sent:
        copy.wait_send()
    for side in sides.values():
        side.wait_send()


def scatter_all(part0, part1, count):
    ups = count // 2
    downs = count - 1 - ups
    block = part0.shape[1:]
    kind = part0.dtype
    return pl.pallas_call(
        lambda *refs: scatter_kernel(count, *refs),
        out_shape=jax.ShapeDtypeStruct(block, jnp.float32),
        in_specs=[pl.BlockSpec(memory_space=pl.ANY)] * 2,
        out_specs=pl.BlockSpec(memory_space=pltpu.VMEM),
        scratch_shapes=[
            pltpu.VMEM((count,) + block, kind),
            pltpu.VMEM((count,) + block, kind),
            pltpu.VMEM((2,) + block, kind),
            pltpu.VMEM((ups,) + block, kind),
            pltpu.VMEM((downs,) + block, kind),
            pltpu.SemaphoreType.DMA,
            pltpu.SemaphoreType.DMA((ups,)),
            pltpu.SemaphoreType.DMA((ups,)),
            pltpu.SemaphoreType.DMA((ups,)),
            pltpu.SemaphoreType.DMA((ups,)),
            pltpu.SemaphoreType.DMA((count,)),
            pltpu.SemaphoreType.DMA((count,)),
        ],
        compiler_params=pltpu.CompilerParams(collective_id=1, has_side_effects=True),
        name="scatter_grads",
    )(part0, part1)


EXTRA = 16


def pack(qkv, proj, up, down, row):
    owners = qkv.shape[0]
    pieces = []
    for matrix in (qkv, proj, up, down):
        for start in range(0, matrix.shape[2], D):
            pieces.append(matrix[:, :, start : start + D])
    row = jnp.pad(row[:, None, :], ((0, 0), (0, EXTRA - 1), (0, D - row.shape[1])))
    return jnp.concatenate(pieces + [row], 1).reshape(owners, -1, D)


def unpack(packed, share):
    start = 0
    matrices = []
    for extent, rows in ((3 * D, share), (D, share), (FF, share), (D, 4 * share)):
        pieces = []
        for _ in range(extent // D):
            pieces.append(packed[start : start + rows])
            start = start + rows
        matrices.append(jnp.concatenate(pieces, 1))
    return matrices


def by_flag(flag, first, second):
    return jnp.where(flag == 0, jnp.stack([first, second]), jnp.stack([second, first]))


def swap_sections(value):
    return lax.ppermute(value, "section", [(0, 1), (1, 0)])


def whole_images(halves, section, half):
    share = halves.shape[1] // (2 * lax.axis_size("section"))
    own = lax.dynamic_slice_in_dim(halves, (section * 2 + half) * share, share, 1)
    away = lax.dynamic_slice_in_dim(halves, (section * 2 + 1 - half) * share, share, 1)
    both = by_flag(half, own, partner(away, "fsdp", 0))
    both = both.transpose(1, 2, 3, 0, 4, 5, 6)
    return both.reshape(both.shape[0], -1, SIDE, SIDE, D)


def spread_images(first, second, section, half, groups):
    mine = jnp.where(section == 0, first, second)
    other = jnp.where(section == 0, second, first)
    both = by_flag(section, mine, swap_sections(other))
    both = both.reshape(both.shape[0], -1, groups, 2, WIN, SIDE, D)
    kept = jnp.where(half == 0, both[:, :, :, 0], both[:, :, :, 1])
    away = jnp.where(half == 0, both[:, :, :, 1], both[:, :, :, 0])
    halves = by_flag(half, kept, partner(away, "fsdp", 0))
    return halves.transpose(1, 0, 2, 3, 4, 5, 6).reshape(-1, groups, WIN, SIDE, D)


def on_device(
    block_input, cotangent, qkv_weight, proj_weight, fc1_weight, fc2_weight, vectors, rel_table
):
    section = lax.axis_index("section")
    sections = lax.axis_size("section")
    half = lax.axis_index("fsdp") % 2
    count = lax.axis_size("fsdp")
    groups = block_input.shape[1]
    share = qkv_weight.shape[1]
    width = vectors.shape[1]
    onehot = relative_onehot()
    gathered = gather_all(
        pack(qkv_weight, proj_weight, fc1_weight, fc2_weight, vectors)[0], sections, count
    )
    images = whole_images(jnp.stack([block_input, cotangent]), section, half)
    tables = by_flag(section, rel_table[0], swap_sections(rel_table[0]))
    biases = (
        score_bias(tables[0], None, onehot),
        score_bias(tables[1], allowed_pairs(), onehot),
    )
    grouped = [regroup(gathered[layer], share) for layer in range(2)]
    rows = gathered[:, :, BLOCKS * share, :width].reshape(2, BLOCKS, D).astype(jnp.float32)
    batch = images.shape[1]
    inputs = [pad_windows(images[0])]
    result = run_forward(inputs[0], grouped[0], rows[0], biases[0])
    first_out, first_saved = unpad_windows(result[0], batch), result[1:]
    inputs.append(pad_windows(jnp.roll(first_out, (-SHIFT, -SHIFT), (1, 2))))
    result = run_forward(inputs[1], grouped[1], rows[1], biases[1])
    second_saved = result[1:]
    second_out = jnp.roll(unpad_windows(result[0], batch), (SHIFT, SHIFT), (1, 2))
    grad = pad_windows(jnp.roll(images[1], (-SHIFT, -SHIFT), (1, 2)).astype(jnp.float32))
    second = run_backward(grad, inputs[1], grouped[1], rows[1], second_saved)
    second_grid = jnp.roll(unpad_windows(second[0], batch), (SHIFT, SHIFT), (1, 2))
    first = run_backward(pad_windows(second_grid), inputs[0], grouped[0], rows[0], first_saved)
    first_grid = unpad_windows(first[0], batch)
    summed = scatter_all(ungroup(first[1], count), ungroup(second[1], count), count)
    mine = unpack(summed, share)
    pair = [
        jnp.concatenate([part[2].reshape(-1), table_sums(part[3], onehot).reshape(-1)])
        for part in (first, second)
    ]
    small = lax.psum(jnp.stack(pair), ("section", "fsdp"))
    small = jnp.where(section == 0, small[0], small[1])
    row = lax.dynamic_slice_in_dim(small, lax.axis_index("fsdp") * width, width)
    table_total = small[BLOCKS * D :].reshape(rel_table.shape[1:])
    produced = spread_images(first_out, second_out, section, half, groups)
    returned = spread_images(
        first_grid.astype(jnp.bfloat16), second_grid.astype(jnp.bfloat16), section, half, groups
    ).astype(jnp.float32)
    return (
        produced[None],
        returned[None],
        mine[0][None],
        mine[1][None],
        mine[2][None],
        mine[3][None],
        row[None],
        table_total[None],
    )


def solution(mesh):
    in_specs = (
        P(None, "fsdp", None, None, None),
        P(None, "fsdp", None, None, None),
        P("section", "fsdp", None),
        P("section", "fsdp", None),
        P("section", "fsdp", None),
        P("section", "fsdp", None),
        P("section", "fsdp"),
        P("section", None, None),
    )
    out_specs = (
        P("section", None, "fsdp", None, None, None),
        P("section", None, "fsdp", None, None, None),
        P("section", "fsdp", None),
        P("section", "fsdp", None),
        P("section", "fsdp", None),
        P("section", "fsdp", None),
        P("section", "fsdp"),
        P("section", None, None),
    )
    return jax.shard_map(
        on_device, mesh=mesh, in_specs=in_specs, out_specs=out_specs, check_vma=False
    )
```
